32 devices in a mesh: dp: 4 (over y, x), feat: 8 (over z, core).
Axes of the slice: x: 2, y: 2, z: 4, core: 2. Of those that a mesh axis runs over, the one named last changes fastest.
Arguments:
- features: bfloat16 [8192, 1024], P('dp', 'feat'), may hold values from -6 to 6
- owners: int32 [8, 64, 1], P('feat', 'dp'), may hold values from 0 to 3; in each aligned block of 16 rows (0 to 15, 16 to 31, ..., all dimensions but the last counted through in order) at most 8 rows name the same one
- weights: bfloat16 [8, 4096], P(None, ('dp', 'feat')), may hold values from -0.1875 to 0.1875
- labels: int32 [8192], P('dp'), may hold values from 0 to 7
Outputs:
- hessian: float32 [32, 1024, 1024], P(('dp', 'feat'))
- gradient: float32 [8, 4096], P(None, ('dp', 'feat'))
The draws below stay inside these ranges and needn't reach their ends.
Inputs may be any that keep to these rules, and one draw needn't show every extreme that they name: `owners`: among the 16 row blocks of one index of dp, in one tile column, at most 8 name the same owner, a bound that some block reaches.
All inputs are finite; a program needn't handle non-finite values.
Results may differ from the reference program's by a relative error of at most 0.0023.
Values may be sent and summed in bfloat16 or wider, within the bound.
A program may use at most 64 MiB of HBM per device.

```python
import math
import jax
import jax.numpy as jnp
import numpy as np
from jax import lax

C = 8
TW = 128
RB = 128
NBD = 16
CAP = 8
ROWS = 8192
NB = 64
NT = 32
F = 4096
N_DP = 4
N_FEAT = 8


def plant(array, own_key, low, high):
    longest = array.shape.index(max(array.shape))
    spots = []
    for shift in (0, 1):
        where = [jax.random.randint(jax.random.fold_in(own_key, axis), (), 0, length) for axis, length in enumerate(array.shape)]
        where[longest] = (where[longest] + shift) % array.shape[longest]
        spots.append(tuple(where))
    return array.at[spots[0]].set(low).at[spots[1]].set(high)


def shard_levels(rng, dims, split, least, high):
    def one(axis_at, shards_of):
        draws = jax.random.uniform(jax.random.fold_in(jax.random.fold_in(rng, 6), axis_at), (shards_of,), jnp.float32, least / len(split), high / len(split))
        return jnp.repeat(jnp.exp(draws), dims[axis_at] // shards_of).reshape((-1,) + (1,) * (len(dims) - axis_at - 1))

    gain = one(*split[0])
    for cut in split[1:]:
        gain = gain * one(*cut)
    return gain


def deal_out(rng, own, number, rows, amount, top, reach, lean):
    sequence = jax.random.permutation(rng, amount)
    crowded, usual = shares(amount, rows * top, reach, lean, True), shares(amount, rows * top, reach, lean, False)
    places = jnp.arange(amount)

    def named(lengths, rotation):
        used = int((lengths > 0).sum())
        fixed = max(1, used // 4)
        shifted = fixed + (places - fixed + rotation * (used - fixed)) % max(1, amount - fixed)
        return jnp.zeros((amount,), jnp.int32).at[sequence[jnp.where(places < fixed, places, shifted)]].set(jnp.asarray(lengths, jnp.int32))

    lengths = jnp.where(number % 4 == 0, named(crowded, number // 4), named(usual, number - number // 4 - 1))
    mixed = jax.random.permutation(jax.random.fold_in(own, 3), amount)
    donor, taker = mixed[0:amount // 2 * 2:2], mixed[1:amount // 2 * 2:2]
    slack = jnp.minimum(lengths[donor] - 1, reach - lengths[taker]) // 2
    slack = jnp.where((donor == sequence[0]) | (taker == sequence[0]) | (lengths[taker] == 0), 0, jnp.maximum(slack, 0))
    shifted = jax.random.randint(jax.random.fold_in(own, 4), (amount // 2,), 0, 1 << 20) % (slack + 1)
    lengths = lengths.at[donor].add(-shifted).at[taker].add(shifted)
    members = jnp.searchsorted(jnp.cumsum(lengths), jnp.arange(rows * top), side="right").astype(jnp.int32)
    table = members.reshape(top, rows).T
    table = table[jax.random.permutation(jax.random.fold_in(own, 1), rows)]
    rotation = jax.random.randint(jax.random.fold_in(own, 2), (rows, 1), 0, top)
    return jnp.take_along_axis(table, (jnp.arange(top)[None, :] + rotation) % top, axis=1)


def shares(amount, total, reach, skew, full):
    loads = [(1 << 20) // math.isqrt(grade ** skew) + 1 for grade in range(1, amount + 1)]
    largest = reach if full else min(reach, max(-(-total // amount), total * loads[0] // sum(loads)))
    least = 1 if total - largest >= amount - 1 else 0
    given, rest = [largest] + [least] * (amount - 1), total - largest - least * (amount - 1)
    while rest > 0:
        candidates = [i for i in range(1, amount) if given[i] < largest] or [i for i in range(1, amount) if given[i] < reach]
        mass, remaining = sum([loads[i] for i in candidates]), rest
        for i in candidates:
            addition = min(reach - given[i], max(1, remaining * loads[i] // mass), rest)
            given[i] = given[i] + addition
            rest = rest - addition
    return np.array(given)


def scatter_about(rng, dims, scale, limit, shards=(), held_as=jnp.bfloat16):
    result = jax.random.normal(rng, dims, jnp.float32) * scale
    if len(shards) > 0:
        result = shard_levels(rng, dims, shards, -0.22, 0.18) * result
    return jnp.clip(result, min=-limit, max=limit).astype(held_as)


def setup_inputs(seed: int = 0) -> dict:
    key_of = jax.random.split(jax.random.key(seed), 5)
    features = scatter_about(key_of[0], (ROWS, N_FEAT * TW), 1.0, 6.0, ((0, 4), (1, 8)))
    owners_keys = jax.random.split(jax.random.fold_in(key_of[1], 1), N_FEAT * NB // NBD)
    owners_turns = jax.random.permutation(jax.random.fold_in(key_of[1], 3), N_FEAT * NB // NBD)
    owners = jax.vmap(lambda own, number: deal_out(jax.random.fold_in(key_of[1], 2), own, number, NBD, N_DP, 1, CAP, 2))(owners_keys, owners_turns).reshape((N_FEAT, NB, 1))
    weights = scatter_about(key_of[2], (C, F), (N_FEAT * TW) ** -0.5, 0.1875, ((1, 32),))
    labels = plant(jax.random.randint(key_of[3], (ROWS,), 0, C), jax.random.fold_in(key_of[3], 1), 0, C - 1).astype(jnp.int32)
    return {"features": features, "owners": owners, "weights": weights, "labels": labels}


def normalize(logits):
    expo = jnp.exp(logits)
    return expo / jnp.sum(expo, axis=-1, keepdims=True)


def spread_diagonal(diag_part, classes, width):
    blocks = diag_part.reshape(classes, width, width)
    unit = jnp.eye(classes, dtype=jnp.float32)
    return (unit[:, None, :, None] * blocks[:, :, None, :]).reshape(classes * width, classes * width)


def reference(features, owners, weights, labels):
    table = weights.reshape(C, NT, TW).astype(jnp.float32)
    logits = jnp.zeros((NB, RB, C), jnp.float32)
    for column in range(N_FEAT):
        values = features[:, column * TW:(column + 1) * TW].reshape(NB, RB, TW).astype(jnp.float32)
        tiles = owners[column, :, 0].astype(jnp.int32) * N_FEAT + column
        chosen = jnp.take(table, tiles, axis=1)
        logits = logits + jnp.einsum('brt,cbt->brc', values, chosen)
    logits = logits.reshape(ROWS, C)
    probs = normalize(logits)
    probs_half = probs.astype(jnp.bfloat16)
    onehot = (labels[:, None] == jnp.arange(C, dtype=jnp.int32)[None, :]).astype(jnp.float32)
    resid = (probs - onehot).astype(jnp.bfloat16)
    flat_owner = owners.reshape(N_FEAT * NB).astype(jnp.int32)

    def visit(step, state):
        hess_acc, grad_acc = state
        column = step // NB
        block = step % NB
        tile = flat_owner[step] * N_FEAT + column
        x_part = lax.dynamic_slice(features, (block * RB, column * TW), (RB, TW))
        p_part = lax.dynamic_slice_in_dim(probs_half, block * RB, RB, 0).astype(jnp.float32)
        r_part = lax.dynamic_slice_in_dim(resid, block * RB, RB, 0)
        kron_rows = (p_part[:, :, None] * x_part.astype(jnp.float32)[:, None, :]).reshape(RB, C * TW).astype(jnp.bfloat16)
        square = lax.dot_general(kron_rows, kron_rows, (((0,), (0,)), ((), ())), preferred_element_type=jnp.float32)
        diag_part = lax.dot_general(kron_rows, x_part, (((0,), (0,)), ((), ())), preferred_element_type=jnp.float32)
        term = spread_diagonal(diag_part, C, TW) - square
        grad_term = lax.dot_general(r_part, x_part, (((0,), (0,)), ((), ())), preferred_element_type=jnp.float32)
        hess_acc = hess_acc.at[tile].add(term)
        grad_acc = grad_acc.at[tile].add(grad_term)
        return hess_acc, grad_acc

    start = (jnp.zeros((NT, C * TW, C * TW), jnp.float32), jnp.zeros((NT, C, TW), jnp.float32))
    hess_acc, grad_acc = lax.fori_loop(0, N_FEAT * NB, visit, start)
    hessian = hess_acc / RB
    gradient = jnp.transpose(grad_acc, (1, 0, 2)).reshape(C, F) / RB
    return hessian, gradient
```

```python
import functools

import jax
import jax.numpy as jnp
from jax import lax
from jax.experimental import pallas as pl
from jax.experimental.pallas import tpu as pltpu
from jax.sharding import PartitionSpec as P

MESH = pl.DeviceIdType.MESH
NT = (((1,), (1,)), ((), ()))


def exchange_kernel(
    dp, feat, capacity,
    owner_ref, x_ref, w_ref, label_ref,
    xt_ref, pt_ref,
    chain, source, table, sent_x, got_x, part, got_part, joint, sent_p, got_p,
    w_send, w_recv, x_send, x_recv, l_send, l_recv, j_send, j_recv, p_send, p_recv,
):
    blocks, block_rows, width = x_ref.shape
    classes = w_ref.shape[0]
    per_feat = blocks // feat
    row = lax.axis_index("dp")
    col = lax.axis_index("feat")

    def dp_peer(offset):
        return (lax.rem(row + offset, dp), col)

    def feat_peer(offset):
        return (row, lax.rem(col + offset, feat))

    barrier = pltpu.get_barrier_semaphore()
    for offset in range(1, dp):
        pl.semaphore_signal(barrier, inc=1, device_id=dp_peer(offset), device_id_type=MESH)
    for offset in range(1, feat):
        pl.semaphore_signal(barrier, inc=1, device_id=feat_peer(offset), device_id_type=MESH)

    heads = [jnp.int32(blocks)] * dp
    chain[blocks] = jnp.int32(blocks)
    for block in reversed(range(blocks)):
        away = lax.rem(owner_ref[block] - row + dp, dp)
        follower = heads[0]
        for offset in range(1, dp):
            follower = jnp.where(away == offset, heads[offset], follower)
        chain[block] = follower
        heads = [jnp.where(away == offset, block, heads[offset]) for offset in range(dp)]
    for offset in range(dp):
        at = heads[offset]
        for k in range(capacity):
            source[offset * capacity + k] = at
            at = chain[at]

    for offset in range(1, dp):
        for k in range(capacity):
            at = jnp.minimum(source[offset * capacity + k], blocks - 1)
            sent_x[offset, k] = x_ref[at]
    table[0] = w_ref[...]

    pl.semaphore_wait(barrier, dp - 1 + feat - 1)

    w_copies, x_copies = [], []
    for offset in range(1, dp):
        copy = pltpu.make_async_remote_copy(
            src_ref=w_ref, dst_ref=table.at[offset],
            send_sem=w_send.at[offset], recv_sem=w_recv.at[offset],
            device_id=dp_peer(offset), device_id_type=MESH,
        )
        copy.start()
        w_copies.append(copy)
    for offset in range(1, dp):
        copy = pltpu.make_async_remote_copy(
            src_ref=sent_x.at[offset], dst_ref=got_x.at[offset],
            send_sem=x_send.at[offset], recv_sem=x_recv.at[offset],
            device_id=dp_peer(offset), device_id_type=MESH,
        )
        copy.start()
        x_copies.append(copy)

    for k in range(capacity):
        at = jnp.minimum(source[k], blocks - 1)
        xt_ref[:, k * block_rows:(k + 1) * block_rows] = x_ref[at].T

    for copy in w_copies:
        copy.wait()

    for block in range(blocks):
        w_block = table[lax.rem(row - owner_ref[block] + dp, dp)]
        part[block] = lax.dot_general(
            w_block, x_ref[block], NT, preferred_element_type=jnp.float32
        )

    l_copies = []
    for offset in range(1, feat):
        to = lax.rem(col + offset, feat)
        copy = pltpu.make_async_remote_copy(
            src_ref=part.at[pl.ds(to * per_feat, per_feat)], dst_ref=got_part.at[offset],
            send_sem=l_send.at[offset], recv_sem=l_recv.at[offset],
            device_id=feat_peer(offset), device_id_type=MESH,
        )
        copy.start()
        l_copies.append(copy)
    for copy in l_copies:
        copy.wait()

    for i in range(per_feat):
        block = col * per_feat + i
        logits = part[block]
        for offset in range(1, feat):
            logits = logits + got_part[offset, i]
        expo = jnp.exp(logits)
        probs = expo / jnp.sum(expo, axis=0, keepdims=True)
        label = label_ref[pl.ds(block, 1), :]
        onehot = lax.broadcasted_iota(jnp.int32, probs.shape, 0) == label
        resid = probs - onehot.astype(jnp.float32)
        joint[block] = jnp.concatenate([probs, resid], axis=0).astype(jnp.bfloat16)

    j_copies = []
    mine = pl.ds(col * per_feat, per_feat)
    for offset in range(1, feat):
        copy = pltpu.make_async_remote_copy(
            src_ref=joint.at[mine], dst_ref=joint.at[mine],
            send_sem=j_send.at[offset], recv_sem=j_recv.at[offset],
            device_id=feat_peer(offset), device_id_type=MESH,
        )
        copy.start()
        j_copies.append(copy)
    for offset in range(1, feat):
        j_copies[offset - 1].wait_send()
        came = lax.rem(col - offset + feat, feat)
        theirs = pl.ds(came * per_feat, per_feat)
        pltpu.make_async_remote_copy(
            src_ref=joint.at[theirs], dst_ref=joint.at[theirs],
            send_sem=j_send.at[offset], recv_sem=j_recv.at[offset],
            device_id=feat_peer(offset), device_id_type=MESH,
        ).wait_recv()

    def picked(offset, k):
        at = source[offset * capacity + k]
        tile = joint[jnp.minimum(at, blocks - 1)]
        return jnp.where(at < blocks, tile, jnp.zeros_like(tile))

    p_copies = []
    for offset in range(1, dp):
        for k in range(capacity):
            sent_p[offset, k] = picked(offset, k)
        copy = pltpu.make_async_remote_copy(
            src_ref=sent_p.at[offset], dst_ref=got_p.at[offset],
            send_sem=p_send.at[offset], recv_sem=p_recv.at[offset],
            device_id=dp_peer(offset), device_id_type=MESH,
        )
        copy.start()
        p_copies.append(copy)
    for k in range(capacity):
        pt_ref[:, k * block_rows:(k + 1) * block_rows] = picked(0, k)

    for offset in range(1, dp):
        x_copies[offset - 1].wait()
        for k in range(capacity):
            begin = (offset * capacity + k) * block_rows
            xt_ref[:, begin:begin + block_rows] = got_x[offset, k].T
    for offset in range(1, dp):
        p_copies[offset - 1].wait()
        for k in range(capacity):
            begin = (offset * capacity + k) * block_rows
            pt_ref[:, begin:begin + block_rows] = got_p[offset, k]


def hessian_kernel(classes, scale, xt_ref, pt_ref, hess_ref, grad_ref, kron, acc, sems):
    width, rows = xt_ref.shape
    pair = 2 * width
    tiles = classes // 2
    lanes = 512

    def build(c):
        for begin in range(0, rows, lanes):
            p_row = pt_ref[c:c + 1, begin:begin + lanes]
            kron[c * width:(c + 1) * width, begin:begin + lanes] = (
                p_row * xt_ref[:, begin:begin + lanes]
            )

    copies = []

    def write(r0, r1, c0, c1):
        copy = pltpu.make_async_copy(
            acc.at[r0:r1, c0:c1], hess_ref.at[0, r0:r1, c0:c1], sems.at[len(copies)]
        )
        copy.start()
        copies.append(copy)

    grad_ref[...] = scale * lax.dot_general(
        pt_ref[...], xt_ref[...], NT, preferred_element_type=jnp.float32
    )[classes:]
    for n in range(tiles):
        build(2 * n)
        build(2 * n + 1)
        low, high = n * pair, (n + 1) * pair
        right = kron[low:high, :]
        for m in range(n + 1):
            square = lax.dot_general(
                kron[m * pair:(m + 1) * pair, :], right, NT, preferred_element_type=jnp.float32
            )
            value = square * (-scale)
            acc[m * pair:(m + 1) * pair, low:high] = value
            if m < n:
                acc[low:high, m * pair:(m + 1) * pair] = value.T
        diag = lax.dot_general(xt_ref[...], right, NT, preferred_element_type=jnp.float32) * scale
        for half in range(2):
            b0 = low + half * width
            acc[b0:b0 + width, b0:b0 + width] += diag[:, half * width:(half + 1) * width].T
        write(0, high, low, high)
        if n > 0:
            write(low, high, 0, low)
    for copy in copies:
        copy.wait()


def per_device(dp, feat, features, owners, weights, labels):
    rows, width = features.shape
    classes = weights.shape[0]
    blocks = owners.shape[1]
    block_rows = rows // blocks
    capacity = max(2, 2 * ((blocks + dp - 1) // dp))
    total = dp * capacity * block_rows
    per_feat = blocks // feat
    bf16, f32 = jnp.bfloat16, jnp.float32
    vmem = pl.BlockSpec(memory_space=pltpu.VMEM)
    dma = pltpu.SemaphoreType.DMA
    x_t, p_t = pl.pallas_call(
        functools.partial(exchange_kernel, dp, feat, capacity),
        out_shape=(
            jax.ShapeDtypeStruct((width, total), bf16),
            jax.ShapeDtypeStruct((2 * classes, total), bf16),
        ),
        in_specs=[pl.BlockSpec(memory_space=pltpu.SMEM), vmem, vmem, vmem],
        out_specs=(vmem, vmem),
        scratch_shapes=[
            pltpu.SMEM((blocks + 1,), jnp.int32),
            pltpu.SMEM((dp * capacity,), jnp.int32),
            pltpu.VMEM((dp, classes, width), bf16),
            pltpu.VMEM((dp, capacity, block_rows, width), bf16),
            pltpu.VMEM((dp, capacity, block_rows, width), bf16),
            pltpu.VMEM((blocks, classes, block_rows), f32),
            pltpu.VMEM((feat, per_feat, classes, block_rows), f32),
            pltpu.VMEM((blocks, 2 * classes, block_rows), bf16),
            pltpu.VMEM((dp, capacity, 2 * classes, block_rows), bf16),
            pltpu.VMEM((dp, capacity, 2 * classes, block_rows), bf16),
            dma((dp,)), dma((dp,)), dma((dp,)), dma((dp,)),
            dma((feat,)), dma((feat,)), dma((feat,)), dma((feat,)),
            dma((dp,)), dma((dp,)),
        ],
        compiler_params=pltpu.CompilerParams(
            collective_id=0, has_side_effects=True, vmem_limit_bytes=24 << 20
        ),
        name="exchange",
    )(
        owners.reshape(blocks),
        features.reshape(blocks, block_rows, width),
        weights,
        labels.reshape(blocks, block_rows),
    )
    size = classes * width
    return pl.pallas_call(
        functools.partial(hessian_kernel, classes, 1.0 / block_rows),
        out_shape=(
            jax.ShapeDtypeStruct((1, size, size), f32),
            jax.ShapeDtypeStruct((classes, width), f32),
        ),
        in_specs=[vmem, vmem],
        out_specs=(pl.BlockSpec(memory_space=pl.ANY), vmem),
        scratch_shapes=[
            pltpu.VMEM((size, total), bf16),
            pltpu.VMEM((size, size), f32),
            dma((classes,)),
        ],
        compiler_params=pltpu.CompilerParams(vmem_limit_bytes=40 << 20),
        name="hessian",
    )(x_t, p_t)


def solution(mesh):
    in_specs = (P("dp", "feat"), P("feat", "dp", None), P(None, ("dp", "feat")), P("dp"))
    out_specs = (P(("dp", "feat"), None, None), P(None, ("dp", "feat")))
    return jax.shard_map(
        functools.partial(per_device, mesh.shape["dp"], mesh.shape["feat"]),
        mesh=mesh, in_specs=in_specs, out_specs=out_specs, check_vma=False,
    )
```

```python
import functools

import jax
import jax.numpy as jnp
from jax import lax
from jax.experimental import pallas as pl
from jax.experimental.pallas import tpu as pltpu
from jax.sharding import PartitionSpec as P

MESH = pl.DeviceIdType.MESH
NT = (((1,), (1,)), ((), ()))


def exchange_kernel(
    dp, feat, capacity,
    owner_ref, x_hbm, w_hbm, label_hbm,
    xt_ref, pt_ref,
    x_ref, label_ref, in_sems, chain, source, table, sent_x, got_x, part, got_part, joint, sent_p, got_p,
    w_send, w_recv, x_send, x_recv, l_send, l_recv, j_send, j_recv, p_send, p_recv,
):
    blocks, block_rows, width = x_ref.shape
    classes = w_hbm.shape[0]
    per_feat = blocks // feat
    row = lax.axis_index("dp")
    col = lax.axis_index("feat")

    def dp_peer(offset):
        return (lax.rem(row + offset, dp), col)

    def feat_peer(offset):
        return (row, lax.rem(col + offset, feat))

    x_load = pltpu.make_async_copy(x_hbm, x_ref, in_sems.at[0])
    w_load = pltpu.make_async_copy(w_hbm, table.at[0], in_sems.at[1])
    label_load = pltpu.make_async_copy(label_hbm, label_ref, in_sems.at[2])
    x_load.start()
    w_load.start()
    label_load.start()
    barrier = pltpu.get_barrier_semaphore()
    for offset in range(1, dp):
        pl.semaphore_signal(barrier, inc=1, device_id=dp_peer(offset), device_id_type=MESH)
    for offset in range(1, feat):
        pl.semaphore_signal(barrier, inc=1, device_id=feat_peer(offset), device_id_type=MESH)

    heads = [jnp.int32(blocks)] * dp
    chain[blocks] = jnp.int32(blocks)
    for block in reversed(range(blocks)):
        away = lax.rem(owner_ref[block] - row + dp, dp)
        follower = heads[0]
        for offset in range(1, dp):
            follower = jnp.where(away == offset, heads[offset], follower)
        chain[block] = follower
        heads = [jnp.where(away == offset, block, heads[offset]) for offset in range(dp)]
    for offset in range(dp):
        at = heads[offset]
        for k in range(capacity):
            source[offset * capacity + k] = at
            at = chain[at]

    x_load.wait()
    w_load.wait()
    label_load.wait()
    for offset in range(1, dp):
        for k in range(capacity):
            at = jnp.minimum(source[offset * capacity + k], blocks - 1)
            sent_x[offset, k] = x_ref[at]

    pl.semaphore_wait(barrier, dp - 1 + feat - 1)

    w_copies, x_copies = [], []
    for offset in range(1, dp):
        copy = pltpu.make_async_remote_copy(
            src_ref=table.at[0], dst_ref=table.at[offset],
            send_sem=w_send.at[offset], recv_sem=w_recv.at[offset],
            device_id=dp_peer(offset), device_id_type=MESH,
        )
        copy.start()
        w_copies.append(copy)
    for offset in range(1, dp):
        copy = pltpu.make_async_remote_copy(
            src_ref=sent_x.at[offset], dst_ref=got_x.at[offset],
            send_sem=x_send.at[offset], recv_sem=x_recv.at[offset],
            device_id=dp_peer(offset), device_id_type=MESH,
        )
        copy.start()
        x_copies.append(copy)

    for k in range(capacity):
        at = jnp.minimum(source[k], blocks - 1)
        xt_ref[:, k * block_rows:(k + 1) * block_rows] = x_ref[at].T

    for copy in w_copies:
        copy.wait()

    for block in range(blocks):
        w_block = table[lax.rem(row - owner_ref[block] + dp, dp)]
        part[block] = lax.dot_general(
            w_block, x_ref[block], NT, preferred_element_type=jnp.float32
        )

    l_copies = []
    for offset in range(1, feat):
        to = lax.rem(col + offset, feat)
        copy = pltpu.make_async_remote_copy(
            src_ref=part.at[pl.ds(to * per_feat, per_feat)], dst_ref=got_part.at[offset],
            send_sem=l_send.at[offset], recv_sem=l_recv.at[offset],
            device_id=feat_peer(offset), device_id_type=MESH,
        )
        copy.start()
        l_copies.append(copy)
    for copy in l_copies:
        copy.wait()

    for i in range(per_feat):
        block = col * per_feat + i
        logits = part[block]
        for offset in range(1, feat):
            logits = logits + got_part[offset, i]
        expo = jnp.exp(logits)
        probs = expo / jnp.sum(expo, axis=0, keepdims=True)
        label = label_ref[pl.ds(block, 1), :]
        onehot = lax.broadcasted_iota(jnp.int32, probs.shape, 0) == label
        resid = probs - onehot.astype(jnp.float32)
        joint[block] = jnp.concatenate([probs, resid], axis=0).astype(jnp.bfloat16)

    j_copies = []
    mine = pl.ds(col * per_feat, per_feat)
    for offset in range(1, feat):
        copy = pltpu.make_async_remote_copy(
            src_ref=joint.at[mine], dst_ref=joint.at[mine],
            send_sem=j_send.at[offset], recv_sem=j_recv.at[offset],
            device_id=feat_peer(offset), device_id_type=MESH,
        )
        copy.start()
        j_copies.append(copy)
    for offset in range(1, feat):
        j_copies[offset - 1].wait_send()
        came = lax.rem(col - offset + feat, feat)
        theirs = pl.ds(came * per_feat, per_feat)
        pltpu.make_async_remote_copy(
            src_ref=joint.at[theirs], dst_ref=joint.at[theirs],
            send_sem=j_send.at[offset], recv_sem=j_recv.at[offset],
            device_id=feat_peer(offset), device_id_type=MESH,
        ).wait_recv()

    def picked(offset, k):
        at = source[offset * capacity + k]
        tile = joint[jnp.minimum(at, blocks - 1)]
        return jnp.where(at < blocks, tile, jnp.zeros_like(tile))

    p_copies = []
    for offset in range(1, dp):
        for k in range(capacity):
            sent_p[offset, k] = picked(offset, k)
        copy = pltpu.make_async_remote_copy(
            src_ref=sent_p.at[offset], dst_ref=got_p.at[offset],
            send_sem=p_send.at[offset], recv_sem=p_recv.at[offset],
            device_id=dp_peer(offset), device_id_type=MESH,
        )
        copy.start()
        p_copies.append(copy)
    for k in range(capacity):
        pt_ref[:, k * block_rows:(k + 1) * block_rows] = picked(0, k)

    for offset in range(1, dp):
        x_copies[offset - 1].wait()
        for k in range(capacity):
            begin = (offset * capacity + k) * block_rows
            xt_ref[:, begin:begin + block_rows] = got_x[offset, k].T
    for offset in range(1, dp):
        p_copies[offset - 1].wait()
        for k in range(capacity):
            begin = (offset * capacity + k) * block_rows
            pt_ref[:, begin:begin + block_rows] = got_p[offset, k]


def hessian_kernel(classes, scale, xt_ref, pt_ref, hess_ref, grad_ref, kron, acc, sems):
    width, rows = xt_ref.shape
    pair = 2 * width
    tiles = classes // 2
    lanes = 512

    def build(c):
        for begin in range(0, rows, lanes):
            p_row = pt_ref[c:c + 1, begin:begin + lanes]
            kron[c * width:(c + 1) * width, begin:begin + lanes] = (
                p_row * xt_ref[:, begin:begin + lanes]
            )

    copies = []

    def write(r0, r1, c0, c1):
        copy = pltpu.make_async_copy(
            acc.at[r0:r1, c0:c1], hess_ref.at[0, r0:r1, c0:c1], sems.at[len(copies)]
        )
        copy.start()
        copies.append(copy)

    grad_ref[...] = scale * lax.dot_general(
        pt_ref[...], xt_ref[...], NT, preferred_element_type=jnp.float32
    )[classes:]
    for n in range(tiles):
        build(2 * n)
        build(2 * n + 1)
        low, high = n * pair, (n + 1) * pair
        right = kron[low:high, :]
        for m in range(n + 1):
            square = lax.dot_general(
                kron[m * pair:(m + 1) * pair, :], right, NT, preferred_element_type=jnp.float32
            )
            value = square * (-scale)
            acc[m * pair:(m + 1) * pair, low:high] = value
            if m < n:
                acc[low:high, m * pair:(m + 1) * pair] = value.T
        diag = lax.dot_general(xt_ref[...], right, NT, preferred_element_type=jnp.float32) * scale
        for half in range(2):
            b0 = low + half * width
            acc[b0:b0 + width, b0:b0 + width] += diag[:, half * width:(half + 1) * width].T
        write(0, high, low, high)
        if n > 0:
            write(low, high, 0, low)
    for copy in copies:
        copy.wait()


def per_device(dp, feat, features, owners, weights, labels):
    rows, width = features.shape
    classes = weights.shape[0]
    blocks = owners.shape[1]
    block_rows = rows // blocks
    capacity = max(2, 2 * ((blocks + dp - 1) // dp))
    total = dp * capacity * block_rows
    per_feat = blocks // feat
    bf16, f32 = jnp.bfloat16, jnp.float32
    vmem = pl.BlockSpec(memory_space=pltpu.VMEM)
    hbm = pl.BlockSpec(memory_space=pltpu.HBM)
    dma = pltpu.SemaphoreType.DMA
    x_t, p_t = pl.pallas_call(
        functools.partial(exchange_kernel, dp, feat, capacity),
        out_shape=(
            jax.ShapeDtypeStruct((width, total), bf16),
            jax.ShapeDtypeStruct((2 * classes, total), bf16),
        ),
        in_specs=[pl.BlockSpec(memory_space=pltpu.SMEM), hbm, hbm, hbm],
        out_specs=(vmem, vmem),
        scratch_shapes=[
            pltpu.VMEM((blocks, block_rows, width), bf16),
            pltpu.VMEM((blocks, block_rows), jnp.int32),
            dma((3,)),
            pltpu.SMEM((blocks + 1,), jnp.int32),
            pltpu.SMEM((dp * capacity,), jnp.int32),
            pltpu.VMEM((dp, classes, width), bf16),
            pltpu.VMEM((dp, capacity, block_rows, width), bf16),
            pltpu.VMEM((dp, capacity, block_rows, width), bf16),
            pltpu.VMEM((blocks, classes, block_rows), f32),
            pltpu.VMEM((feat, per_feat, classes, block_rows), f32),
            pltpu.VMEM((blocks, 2 * classes, block_rows), bf16),
            pltpu.VMEM((dp, capacity, 2 * classes, block_rows), bf16),
            pltpu.VMEM((dp, capacity, 2 * classes, block_rows), bf16),
            dma((dp,)), dma((dp,)), dma((dp,)), dma((dp,)),
            dma((feat,)), dma((feat,)), dma((feat,)), dma((feat,)),
            dma((dp,)), dma((dp,)),
        ],
        compiler_params=pltpu.CompilerParams(
            collective_id=0, has_side_effects=True, vmem_limit_bytes=24 << 20
        ),
        name="exchange",
    )(
        owners.reshape(blocks),
        features.reshape(blocks, block_rows, width),
        weights,
        labels.reshape(blocks, block_rows),
    )
    size = classes * width
    return pl.pallas_call(
        functools.partial(hessian_kernel, classes, 1.0 / block_rows),
        out_shape=(
            jax.ShapeDtypeStruct((1, size, size), f32),
            jax.ShapeDtypeStruct((classes, width), f32),
        ),
        in_specs=[vmem, vmem],
        out_specs=(pl.BlockSpec(memory_space=pl.ANY), vmem),
        scratch_shapes=[
            pltpu.VMEM((size, total), bf16),
            pltpu.VMEM((size, size), f32),
            dma((classes,)),
        ],
        compiler_params=pltpu.CompilerParams(vmem_limit_bytes=40 << 20),
        name="hessian",
    )(x_t, p_t)


def solution(mesh):
    in_specs = (P("dp", "feat"), P("feat", "dp", None), P(None, ("dp", "feat")), P("dp"))
    out_specs = (P(("dp", "feat"), None, None), P(None, ("dp", "feat")))
    return jax.shard_map(
        functools.partial(per_device, mesh.shape["dp"], mesh.shape["feat"]),
        mesh=mesh, in_specs=in_specs, out_specs=out_specs, check_vma=False,
    )
```
